32 devices in a mesh: row: 8 (over y, x, core), col: 4 (over z).
Axes of the slice: x: 2, y: 2, z: 4, core: 2. Of those that a mesh axis runs over, the one named last changes fastest.
Arguments:
- integrals: float32 [262144, 1024], P(('row', 'col')), may hold values from -0.1875 to 0.1875
- amplitudes: float32 [64, 32768], P(None, ('row', 'col')), may hold values from -6 to 6
Outputs:
- ladder: float32 [16384, 32768], P('row', 'col')
The draws below stay inside these ranges and needn't reach their ends.
All inputs are finite; a program needn't handle non-finite values.
Results may differ from the reference program's by a relative error of at most 0.00007.
Values sent between devices are 32-bit elements; how exact they have to be, the bound alone decides.
No kernel may reach another device: no remote copies, remote signals or barrier semaphores. Data moves between devices by JAX's collectives and lax.ppermute only.
A program may use at most 448 MiB of HBM per device.

```python
import jax
import jax.numpy as jnp
from jax import lax

NV = 512
NO = 64
NI = 32
NC = 2


def steps_of(stream_key, dims, shards, least, top_value):
    def one(position, blocks):
        steps = jax.random.uniform(jax.random.fold_in(jax.random.fold_in(stream_key, 6), position), (blocks,), jnp.float32, least / len(shards), top_value / len(shards))
        return jnp.repeat(jnp.exp(steps), dims[position] // blocks).reshape((-1,) + (1,) * (len(dims) - position - 1))

    level = one(*shards[0])
    for cut in shards[1:]:
        level = level * one(*cut)
    return level


def centred(rng, dims, scale, bound, pieces=(), held_as=jnp.bfloat16):
    factor_of = steps_of(rng, dims, pieces, -0.22, 0.18) if pieces else 1.0
    values = jax.random.normal(rng, dims, jnp.float32) * scale * factor_of
    return jnp.minimum(jnp.maximum(values, -bound), bound).astype(held_as)


def setup_inputs(seed: int = 0) -> dict:
    streams_of = jax.random.split(jax.random.key(seed), 3)
    integrals = centred(streams_of[0], (NV * NV, NC * NV), (NC * NV) ** -0.5, 0.1875, ((0, 32),), jnp.float32)
    amplitudes = centred(streams_of[1], (NC * NI, NV * NO), 1.0, 6.0, ((1, 32),), jnp.float32)
    return dict(integrals=integrals, amplitudes=amplitudes)


def reference(integrals, amplitudes):
    panel_amps = amplitudes.reshape(NC, NI, NV, NO).transpose(0, 2, 1, 3).reshape(NC * NV, NI * NO)
    products = jnp.dot(integrals, panel_amps, precision=lax.Precision.HIGHEST, preferred_element_type=jnp.float32)
    return products.reshape(NV, NV, NI, NO).transpose(0, 2, 1, 3).reshape(NV * NI, NV * NO)
```

```python
import functools

import jax
import jax.numpy as jnp
from jax import lax
from jax.experimental import pallas as pl
from jax.experimental.pallas import tpu as pltpu
from jax.sharding import PartitionSpec as P


NV = 512
NO = 64
NI = 32
NC = 2
LANES = 128
SUBLANES = 8


def split(values):
    high = values.astype(jnp.bfloat16)
    low = (values - high.astype(jnp.float32)).astype(jnp.bfloat16)
    return high, low


def ladder_kernel(group, at_ref, v_ref, th_ref, tl_ref, *refs):
    o_ref, part_ref = refs[-2:]
    b_width, depth = v_ref.shape[2:]
    half = b_width // 2
    rows = group * half
    vh, vl = split(v_ref[...].reshape(group * b_width, depth))
    width = SUBLANES * NO
    low_half = lax.broadcasted_iota(jnp.int32, (rows, LANES), 1) < NO

    @pl.loop(0, NI // SUBLANES)
    def _(n):
        columns = pl.ds(pl.multiple_of(n * width, width), width)
        th, tl = th_ref[:, columns], tl_ref[:, columns]
        dot = functools.partial(jnp.dot, preferred_element_type=jnp.float32)
        acc = dot(vh, tl) + dot(vl, th) + dot(vh, th)
        for pair in range(SUBLANES // 2):
            part_ref[pair] = acc[:, pair * LANES : (pair + 1) * LANES]
            even = part_ref[pair, pl.ds(0, rows, stride=2), :]
            odd = part_ref[pair, pl.ds(1, rows, stride=2), :]
            first = jnp.where(low_half, even, pltpu.roll(odd, NO, axis=1))
            second = jnp.where(low_half, pltpu.roll(even, NO, axis=1), odd)
            for a in range(group):
                base = (a * (NI // SUBLANES) + n) * half * SUBLANES + 2 * pair
                o_ref[pl.ds(base, half, stride=SUBLANES), :] = first[a * half : (a + 1) * half]
                o_ref[pl.ds(base + 1, half, stride=SUBLANES), :] = second[a * half : (a + 1) * half]


def multiply(at, integrals, th, tl, ladder, out_shape):
    avals, _, b_width, depth = integrals.shape
    group = 2 if avals % 2 == 0 else 1
    block_rows = group * NI * b_width * NO // LANES
    aliased = ladder is not None
    spec = pl.BlockSpec((depth, NI * NO), lambda g, at: (0, 0), pipeline_mode=pl.Buffered(1))
    products = avals * b_width * depth * NI * NO
    return pl.pallas_call(
        functools.partial(ladder_kernel, group),
        out_shape=out_shape,
        grid_spec=pltpu.PrefetchScalarGridSpec(
            num_scalar_prefetch=1,
            grid=(avals // group,),
            in_specs=[
                pl.BlockSpec((group, 1, b_width, depth), lambda g, at: (g, at[1], 0, 0)),
                spec,
                spec,
            ]
            + [pl.BlockSpec(memory_space=pl.ANY)] * aliased,
            out_specs=pl.BlockSpec((block_rows, LANES), lambda g, at: (at[0] // group + g, 0)),
            scratch_shapes=[pltpu.VMEM((SUBLANES // 2, group * b_width, LANES), jnp.float32)],
        ),
        input_output_aliases={4: 0} if aliased else {},
        compiler_params=pltpu.CompilerParams(vmem_limit_bytes=40 << 20),
        cost_estimate=pl.CostEstimate(
            flops=6 * products,
            bytes_accessed=4 * (integrals.size + avals * b_width * NI * NO + depth * NI * NO),
            transcendentals=0,
        ),
    )(at, integrals, th, tl, *([ladder] if aliased else []))


def gather_over(axis, pieces, masks):
    size = lax.axis_size(axis)
    here = lax.axis_index(axis)
    held = {0: pieces}
    for mask in masks:
        sent = sorted(held)
        block = jnp.concatenate([held[k] for k in sent]) if len(sent) > 1 else held[sent[0]]
        got = lax.ppermute(block, axis, [(k, k ^ mask) for k in range(size)])
        each = pieces.shape[0]
        for n, k in enumerate(sent):
            held[k ^ mask] = got[n * each : (n + 1) * each]
    stacked = jnp.stack([held[k] for k in range(size)])
    bit = 1
    while bit < size:
        view = stacked.reshape((size // (2 * bit), 2, bit) + pieces.shape)
        stacked = jnp.where((here & bit) != 0, view[:, ::-1], view).reshape((size,) + pieces.shape)
        bit *= 2
    return stacked.reshape((size * pieces.shape[0],) + pieces.shape[1:])


def gather_amplitudes(amplitudes):
    cols, rows = lax.axis_size("col"), lax.axis_size("row")
    bits = [1 << k for k in range((cols - 1).bit_length())]
    masks = ([cols - 1] + bits[:-1]) if cols > 1 else []
    pieces = gather_over("col", amplitudes[None], masks)
    pieces = gather_over("row", pieces, [1 << k for k in range((rows - 1).bit_length())])
    each = amplitudes.shape[1] // NO
    panel = pieces.reshape(-1, NC, NI, each, NO).transpose(1, 0, 3, 2, 4)
    return panel.reshape(NC * NV, NI * NO)


def chunks_of(avals):
    if avals < 16:
        return [1] * avals
    unit = avals // 8
    return [unit, 2 * unit, 2 * unit, 2 * unit, unit]


def body(integrals, amplitudes):
    cols = lax.axis_size("col")
    here = lax.axis_index("col")
    avals = integrals.shape[0] // NV
    b_width = NV // cols
    depth = integrals.shape[1]
    blocks = integrals.reshape(avals, cols, b_width, depth)

    shifts = [s for pair in zip(range(1, cols), range(cols - 1, 0, -1)) for s in pair]
    shifts = list(dict.fromkeys(shifts))
    arrived = []
    start = 0
    source = blocks
    for count in chunks_of(avals):
        pieces = [
            lax.dynamic_slice(source, (start, (here + shift) % cols, 0, 0), (count, 1, b_width, depth))
            for shift in shifts
        ]
        source, *pieces = lax.optimization_barrier((source, *pieces))
        for shift, piece in zip(shifts, pieces):
            got = lax.ppermute(piece, "col", [(k, (k + shift) % cols) for k in range(cols)])
            arrived.append(((here - shift) % cols * avals + start, got))
        start += count

    panel = gather_amplitudes(amplitudes)
    rounded = lax.reduce_precision(panel, 8, 7)
    th, tl = rounded.astype(jnp.bfloat16), (panel - rounded).astype(jnp.bfloat16)

    rows = cols * avals * NI
    tiles = rows * b_width * NO // LANES
    out_shape = jax.ShapeDtypeStruct((tiles, LANES), jnp.float32)
    ladder = multiply(jnp.stack([here * avals, here]), blocks, th, tl, None, out_shape)
    for at, got in arrived:
        ladder = multiply(jnp.stack([at, jnp.zeros_like(at)]), got, th, tl, ladder, out_shape)
    ladder = ladder.reshape(rows // SUBLANES, b_width * NO // LANES, SUBLANES, LANES)
    return ladder.transpose(0, 2, 1, 3).reshape(rows, b_width * NO)


def solution(mesh):
    return jax.shard_map(
        body,
        mesh=mesh,
        in_specs=(P(("row", "col"), None), P(None, ("row", "col"))),
        out_specs=P("row", "col"),
        check_vma=False,
    )
```

```python
import functools

import jax
import jax.numpy as jnp
from jax import lax
from jax.experimental import pallas as pl
from jax.experimental.pallas import tpu as pltpu
from jax.sharding import PartitionSpec as P


NV = 512
NO = 64
NI = 32
NC = 2
LANES = 128
SUBLANES = 8
WIDTH = 256


def split(values):
    high = values.astype(jnp.bfloat16)
    low = (values - high.astype(jnp.float32)).astype(jnp.bfloat16)
    return high, low


def ladder_kernel(group, at_ref, v_ref, th_ref, tl_ref, *refs):
    o_ref, vh_ref, vl_ref, part_ref = refs[-4:]
    b_width, depth = v_ref.shape[2:]
    half = b_width // 2
    rows = group * half

    @pl.when(pl.program_id(1) == 0)
    def _():
        vh_ref[...], vl_ref[...] = split(v_ref[...].reshape(group * b_width, depth))

    pairs = WIDTH // LANES
    low_half = lax.broadcasted_iota(jnp.int32, (rows, LANES), 1) < NO

    @pl.loop(0, SUBLANES * NO // WIDTH)
    def _(n):
        columns = pl.ds(pl.multiple_of(n * WIDTH, WIDTH), WIDTH)
        th, tl = th_ref[:, columns], tl_ref[:, columns]
        vh, vl = vh_ref[...], vl_ref[...]
        dot = functools.partial(jnp.dot, preferred_element_type=jnp.float32)
        acc = dot(vh, tl) + dot(vl, th) + dot(vh, th)
        for pair in range(pairs):
            part_ref[pair] = acc[:, pair * LANES : (pair + 1) * LANES]
            even = part_ref[pair, pl.ds(0, rows, stride=2), :]
            odd = part_ref[pair, pl.ds(1, rows, stride=2), :]
            first = jnp.where(low_half, even, pltpu.roll(odd, NO, axis=1))
            second = jnp.where(low_half, pltpu.roll(even, NO, axis=1), odd)
            i = 2 * (n * pairs + pair)
            for a in range(group):
                o_ref[a, pl.ds(i, half, stride=SUBLANES), :] = first[a * half : (a + 1) * half]
                o_ref[a, pl.ds(i + 1, half, stride=SUBLANES), :] = second[a * half : (a + 1) * half]


def multiply(at, integrals, th, tl, ladder, out_shape):
    avals, _, b_width, depth = integrals.shape
    group = 2 if avals % 2 == 0 else 1
    aliased = ladder is not None
    columns = SUBLANES * NO
    spec = pl.BlockSpec((depth, columns), lambda g, n, at: (0, n))
    products = avals * b_width * depth * NI * NO
    return pl.pallas_call(
        functools.partial(ladder_kernel, group),
        out_shape=out_shape,
        grid_spec=pltpu.PrefetchScalarGridSpec(
            num_scalar_prefetch=1,
            grid=(avals // group, NI // SUBLANES),
            in_specs=[
                pl.BlockSpec((group, 1, b_width, depth), lambda g, n, at: (g, at[1], 0, 0)),
                spec,
                spec,
            ]
            + [pl.BlockSpec(memory_space=pl.ANY)] * aliased,
            out_specs=pl.BlockSpec(
                (group, columns * b_width // LANES, LANES), lambda g, n, at: (at[0] // group + g, n, 0)
            ),
            scratch_shapes=[pltpu.VMEM((group * b_width, depth), jnp.bfloat16)] * 2
            + [pltpu.VMEM((WIDTH // LANES, group * b_width, LANES), jnp.float32)],
        ),
        input_output_aliases={4: 0} if aliased else {},
        compiler_params=pltpu.CompilerParams(vmem_limit_bytes=32 << 20),
        cost_estimate=pl.CostEstimate(
            flops=6 * products,
            bytes_accessed=4 * (integrals.size + avals * b_width * NI * NO + depth * NI * NO),
            transcendentals=0,
        ),
    )(at, integrals, th, tl, *([ladder] if aliased else []))


def gather_over(axis, pieces, masks):
    size = lax.axis_size(axis)
    here = lax.axis_index(axis)
    held = {0: pieces}
    for mask in masks:
        sent = sorted(held)
        block = jnp.concatenate([held[k] for k in sent]) if len(sent) > 1 else held[sent[0]]
        got = lax.ppermute(block, axis, [(k, k ^ mask) for k in range(size)])
        each = pieces.shape[0]
        for n, k in enumerate(sent):
            held[k ^ mask] = got[n * each : (n + 1) * each]
    stacked = jnp.stack([held[k] for k in range(size)])
    bit = 1
    while bit < size:
        view = stacked.reshape((size // (2 * bit), 2, bit) + pieces.shape)
        stacked = jnp.where((here & bit) != 0, view[:, ::-1], view).reshape((size,) + pieces.shape)
        bit *= 2
    return stacked.reshape((size * pieces.shape[0],) + pieces.shape[1:])


def gather_amplitudes(amplitudes):
    cols, rows = lax.axis_size("col"), lax.axis_size("row")
    bits = [1 << k for k in range((cols - 1).bit_length())]
    masks = ([cols - 1] + bits[:-1]) if cols > 1 else []
    pieces = gather_over("col", amplitudes[None], masks)
    pieces = gather_over("row", pieces, [1 << k for k in range((rows - 1).bit_length())])
    each = amplitudes.shape[1] // NO
    panel = pieces.reshape(-1, NC, NI, each, NO).transpose(1, 0, 3, 2, 4)
    return panel.reshape(NC * NV, NI * NO)


def chunks_of(avals):
    if avals < 16:
        return [1] * avals
    unit = avals // 16
    return [unit * count for count in (2, 2, 4, 4, 2, 1, 1)]


def body(integrals, amplitudes):
    cols = lax.axis_size("col")
    here = lax.axis_index("col")
    avals = integrals.shape[0] // NV
    b_width = NV // cols
    depth = integrals.shape[1]
    blocks = integrals.reshape(avals, cols, b_width, depth)

    shifts = [s for pair in zip(range(1, cols), range(cols - 1, 0, -1)) for s in pair]
    shifts = list(dict.fromkeys(shifts))
    arrived = []
    start = 0
    source = blocks
    for count in chunks_of(avals):
        pieces = [
            lax.dynamic_slice(source, (start, (here + shift) % cols, 0, 0), (count, 1, b_width, depth))
            for shift in shifts
        ]
        source, *pieces = lax.optimization_barrier((source, *pieces))
        for shift, piece in zip(shifts, pieces):
            got = lax.ppermute(piece, "col", [(k, (k + shift) % cols) for k in range(cols)])
            arrived.append(((here - shift) % cols * avals + start, got))
        start += count

    panel = gather_amplitudes(amplitudes)
    rounded = lax.reduce_precision(panel, 8, 7)
    th, tl = rounded.astype(jnp.bfloat16), (panel - rounded).astype(jnp.bfloat16)

    rows = cols * avals * NI
    out_shape = jax.ShapeDtypeStruct((cols * avals, NI * b_width * NO // LANES, LANES), jnp.float32)
    ladder = multiply(jnp.stack([here * avals, here]), blocks, th, tl, None, out_shape)
    for at, got in arrived:
        ladder = multiply(jnp.stack([at, jnp.zeros_like(at)]), got, th, tl, ladder, out_shape)
    ladder = ladder.reshape(rows // SUBLANES, b_width * NO // LANES, SUBLANES, LANES)
    return ladder.transpose(0, 2, 1, 3).reshape(rows, b_width * NO)


def solution(mesh):
    return jax.shard_map(
        body,
        mesh=mesh,
        in_specs=(P(("row", "col"), None), P(None, ("row", "col"))),
        out_specs=P("row", "col"),
        check_vma=False,
    )
```

```python
import functools

import jax
import jax.numpy as jnp
from jax import lax
from jax.experimental import pallas as pl
from jax.experimental.pallas import tpu as pltpu
from jax.sharding import PartitionSpec as P


NV = 512
NO = 64
NI = 32
NC = 2
LANES = 128
SUBLANES = 8


def split(values):
    high = values.astype(jnp.bfloat16)
    low = (values - high.astype(jnp.float32)).astype(jnp.bfloat16)
    return high, low


def ladder_kernel(group, width, at_ref, v_ref, th_ref, tl_ref, *refs):
    o_ref, vh_ref, vl_ref, part_ref = refs[-4:]
    b_width, depth = v_ref.shape[2:]
    half = b_width // 2
    rows = group * half
    vh_ref[...], vl_ref[...] = split(v_ref[...].reshape(group * b_width, depth))
    low_half = lax.broadcasted_iota(jnp.int32, (rows, LANES), 1) < NO

    def step(n, columns):
        th, tl = th_ref[:, columns], tl_ref[:, columns]
        vh, vl = vh_ref[...], vl_ref[...]
        dot = functools.partial(jnp.dot, preferred_element_type=jnp.float32)
        acc = dot(vh, tl) + dot(vl, th) + dot(vh, th)
        for pair in range(width // LANES):
            part_ref[pair] = acc[:, pair * LANES : (pair + 1) * LANES]
            even = part_ref[pair, pl.ds(0, rows, stride=2), :]
            odd = part_ref[pair, pl.ds(1, rows, stride=2), :]
            first = jnp.where(low_half, even, pltpu.roll(odd, NO, axis=1))
            second = jnp.where(low_half, pltpu.roll(even, NO, axis=1), odd)
            block, i = divmod(2 * pair, SUBLANES)
            at = (n * (width // (SUBLANES * NO)) + block) * half * SUBLANES + i
            for a in range(group):
                o_ref[a, pl.ds(at, half, stride=SUBLANES), :] = first[a * half : (a + 1) * half]
                o_ref[a, pl.ds(at + 1, half, stride=SUBLANES), :] = second[a * half : (a + 1) * half]

    steps = NI * NO // width
    if steps == 1:
        step(0, slice(None))
    else:

        @pl.loop(0, steps)
        def _(n):
            step(n, pl.ds(pl.multiple_of(n * width, width), width))


def multiply(at, integrals, th, tl, ladder, out_shape, width=SUBLANES * NO):
    avals, _, b_width, depth = integrals.shape
    group = 2 if avals % 2 == 0 else 1
    aliased = ladder is not None
    spec = pl.BlockSpec((depth, NI * NO), lambda g, at: (0, 0), pipeline_mode=pl.Buffered(1))
    products = avals * b_width * depth * NI * NO
    return pl.pallas_call(
        functools.partial(ladder_kernel, group, width),
        out_shape=out_shape,
        grid_spec=pltpu.PrefetchScalarGridSpec(
            num_scalar_prefetch=1,
            grid=(avals // group,),
            in_specs=[
                pl.BlockSpec((group, 1, b_width, depth), lambda g, at: (g, at[1], 0, 0)),
                spec,
                spec,
            ]
            + [pl.BlockSpec(memory_space=pl.ANY)] * aliased,
            out_specs=pl.BlockSpec((group,) + out_shape.shape[1:], lambda g, at: (at[0] // group + g, 0, 0)),
            scratch_shapes=[pltpu.VMEM((group * b_width, depth), jnp.bfloat16)] * 2
            + [pltpu.VMEM((width // LANES, group * b_width, LANES), jnp.float32)],
        ),
        input_output_aliases={4: 0} if aliased else {},
        compiler_params=pltpu.CompilerParams(vmem_limit_bytes=32 << 20),
        cost_estimate=pl.CostEstimate(
            flops=6 * products,
            bytes_accessed=4 * (integrals.size + avals * b_width * NI * NO + depth * NI * NO),
            transcendentals=0,
        ),
    )(at, integrals, th, tl, *([ladder] if aliased else []))


def gather_over(axis, pieces, masks):
    size = lax.axis_size(axis)
    here = lax.axis_index(axis)
    held = {0: pieces}
    for mask in masks:
        sent = sorted(held)
        block = jnp.concatenate([held[k] for k in sent]) if len(sent) > 1 else held[sent[0]]
        got = lax.ppermute(block, axis, [(k, k ^ mask) for k in range(size)])
        each = pieces.shape[0]
        for n, k in enumerate(sent):
            held[k ^ mask] = got[n * each : (n + 1) * each]
    stacked = jnp.stack([held[k] for k in range(size)])
    bit = 1
    while bit < size:
        view = stacked.reshape((size // (2 * bit), 2, bit) + pieces.shape)
        stacked = jnp.where((here & bit) != 0, view[:, ::-1], view).reshape((size,) + pieces.shape)
        bit *= 2
    return stacked.reshape((size * pieces.shape[0],) + pieces.shape[1:])


def gather_amplitudes(amplitudes):
    cols, rows = lax.axis_size("col"), lax.axis_size("row")
    bits = [1 << k for k in range((cols - 1).bit_length())]
    masks = ([cols - 1] + bits[:-1]) if cols > 1 else []
    pieces = gather_over("col", amplitudes[None], masks)
    pieces = gather_over("row", pieces, [1 << k for k in range((rows - 1).bit_length())])
    each = amplitudes.shape[1] // NO
    panel = pieces.reshape(-1, NC, NI, each, NO).transpose(1, 0, 3, 2, 4)
    return panel.reshape(NC * NV, NI * NO)


def rounds_of(avals, cols):
    shifts = [s for pair in zip(range(1, cols), range(cols - 1, 0, -1)) for s in pair]
    shifts = list(dict.fromkeys(shifts))
    if avals < 16:
        sizes = [2] * (avals // 2 - 1) + [1, 1] if avals % 2 == 0 else [1] * avals
        return [[(shift, sum(sizes[:k]), sizes[k]) for shift in shifts] for k in range(len(sizes))]
    unit = avals // 16
    rounds = [[(shift, start * unit, count * unit) for shift in shifts] for start, count in ((0, 2), (2, 2), (4, 4))]
    rounds.append([(shift, 8 * unit, 8 * unit) for shift in shifts[:-1]] + [(shifts[-1], 8 * unit, 4 * unit)])
    rounds += [[(shifts[-1], start * unit, count * unit)] for start, count in ((12, 2), (14, 1), (15, 1))]
    return rounds


def body(integrals, amplitudes):
    cols = lax.axis_size("col")
    here = lax.axis_index("col")
    avals = integrals.shape[0] // NV
    b_width = NV // cols
    depth = integrals.shape[1]
    blocks = integrals.reshape(avals, cols, b_width, depth)

    arrived = []
    source = blocks
    for exchanges in rounds_of(avals, cols):
        pieces = [
            lax.dynamic_slice(source, (start, (here + shift) % cols, 0, 0), (count, 1, b_width, depth))
            for shift, start, count in exchanges
        ]
        source, *pieces = lax.optimization_barrier((source, *pieces))
        for (shift, start, count), piece in zip(exchanges, pieces):
            got = lax.ppermute(piece, "col", [(k, (k + shift) % cols) for k in range(cols)])
            width = NI * NO if len(exchanges) == 1 and count == 1 else SUBLANES * NO
            arrived.append(((here - shift) % cols * avals + start, got, width))

    panel = gather_amplitudes(amplitudes)
    rounded = lax.reduce_precision(panel, 8, 7)
    th, tl = rounded.astype(jnp.bfloat16), (panel - rounded).astype(jnp.bfloat16)

    rows = cols * avals * NI
    out_shape = jax.ShapeDtypeStruct((cols * avals, NI * b_width * NO // LANES, LANES), jnp.float32)
    ladder = multiply(jnp.stack([here * avals, here]), blocks, th, tl, None, out_shape)
    for at, got, width in arrived:
        ladder = multiply(jnp.stack([at, jnp.zeros_like(at)]), got, th, tl, ladder, out_shape, width)
    ladder = ladder.reshape(rows // SUBLANES, b_width * NO // LANES, SUBLANES, LANES)
    return ladder.transpose(0, 2, 1, 3).reshape(rows, b_width * NO)


def solution(mesh):
    return jax.shard_map(
        body,
        mesh=mesh,
        in_specs=(P(("row", "col"), None), P(None, ("row", "col"))),
        out_specs=P("row", "col"),
        check_vma=False,
    )
```

```python
import functools

import jax
import jax.numpy as jnp
from jax import lax
from jax.experimental import pallas as pl
from jax.experimental.pallas import tpu as pltpu
from jax.sharding import PartitionSpec as P


NV = 512
NO = 64
NI = 32
NC = 2
LANES = 128
SUBLANES = 8


def split(values):
    high = values.astype(jnp.bfloat16)
    low = (values - high.astype(jnp.float32)).astype(jnp.bfloat16)
    return high, low


def ladder_kernel(group, width, at_ref, v_ref, th_ref, tl_ref, *refs):
    o_ref, vh_ref, vl_ref, part_ref = refs[-4:]
    b_width, depth = v_ref.shape[2:]
    half = b_width // 2
    rows = group * half
    vh_ref[...], vl_ref[...] = split(v_ref[...].reshape(group * b_width, depth))
    low_half = lax.broadcasted_iota(jnp.int32, (rows, LANES), 1) < NO

    def step(n, columns):
        th, tl = th_ref[:, columns], tl_ref[:, columns]
        vh, vl = vh_ref[...], vl_ref[...]
        dot = functools.partial(jnp.dot, preferred_element_type=jnp.float32)
        acc = dot(vh, tl) + dot(vl, th) + dot(vh, th)
        for pair in range(width // LANES):
            part_ref[pair] = acc[:, pair * LANES : (pair + 1) * LANES]
            even = part_ref[pair, pl.ds(0, rows, stride=2), :]
            odd = part_ref[pair, pl.ds(1, rows, stride=2), :]
            first = jnp.where(low_half, even, pltpu.roll(odd, NO, axis=1))
            second = jnp.where(low_half, pltpu.roll(even, NO, axis=1), odd)
            block, i = divmod(2 * pair, SUBLANES)
            at = (n * (width // (SUBLANES * NO)) + block) * half * SUBLANES + i
            for a in range(group):
                o_ref[a, pl.ds(at, half, stride=SUBLANES), :] = first[a * half : (a + 1) * half]
                o_ref[a, pl.ds(at + 1, half, stride=SUBLANES), :] = second[a * half : (a + 1) * half]

    steps = NI * NO // width
    if steps == 1:
        step(0, slice(None))
    else:

        @pl.loop(0, steps)
        def _(n):
            step(n, pl.ds(pl.multiple_of(n * width, width), width))


def multiply(at, integrals, th, tl, ladder, out_shape):
    avals, _, b_width, depth = integrals.shape
    group = 2 if avals % 2 == 0 else 1
    width = SUBLANES * NO
    aliased = ladder is not None
    spec = pl.BlockSpec((depth, NI * NO), lambda g, at: (0, 0), pipeline_mode=pl.Buffered(1))
    products = avals * b_width * depth * NI * NO
    return pl.pallas_call(
        functools.partial(ladder_kernel, group, width),
        out_shape=out_shape,
        grid_spec=pltpu.PrefetchScalarGridSpec(
            num_scalar_prefetch=1,
            grid=(avals // group,),
            in_specs=[
                pl.BlockSpec((group, 1, b_width, depth), lambda g, at: (g, at[1], 0, 0)),
                spec,
                spec,
            ]
            + [pl.BlockSpec(memory_space=pl.ANY)] * aliased,
            out_specs=pl.BlockSpec((group,) + out_shape.shape[1:], lambda g, at: (at[0] // group + g, 0, 0)),
            scratch_shapes=[pltpu.VMEM((group * b_width, depth), jnp.bfloat16)] * 2
            + [pltpu.VMEM((width // LANES, group * b_width, LANES), jnp.float32)],
        ),
        input_output_aliases={4: 0} if aliased else {},
        compiler_params=pltpu.CompilerParams(vmem_limit_bytes=32 << 20),
        cost_estimate=pl.CostEstimate(
            flops=6 * products,
            bytes_accessed=4 * (integrals.size + avals * b_width * NI * NO + depth * NI * NO),
            transcendentals=0,
        ),
    )(at, integrals, th, tl, *([ladder] if aliased else []))


def last_kernel(part, parts, at_ref, v_ref, th_ref, tl_ref, _, o_ref, vs_ref, part_ref, tile_ref, sems):
    b_width, depth = v_ref.shape[2:]
    half = b_width // 2
    vs_ref[:b_width, :], vs_ref[b_width:, :] = split(v_ref[...].reshape(b_width, depth))
    dot = functools.partial(jnp.dot, preferred_element_type=jnp.float32)
    both = dot(vs_ref[...], th_ref[...])
    acc = dot(vs_ref[:b_width, :], tl_ref[...]) + both[b_width:] + both[:b_width]
    low_half = lax.broadcasted_iota(jnp.int32, (half, LANES), 1) < NO
    copies = []
    for pair in range(NI * NO // LANES):
        part_ref[pair] = acc[:, pair * LANES : (pair + 1) * LANES]
        even = part_ref[pair, pl.ds(0, half, stride=2), :]
        odd = part_ref[pair, pl.ds(1, half, stride=2), :]
        block, i = divmod(2 * pair, SUBLANES)
        at = block * half * SUBLANES + i
        tile_ref[pl.ds(at, half, stride=SUBLANES), :] = jnp.where(low_half, even, pltpu.roll(odd, NO, axis=1))
        tile_ref[pl.ds(at + 1, half, stride=SUBLANES), :] = jnp.where(low_half, pltpu.roll(even, NO, axis=1), odd)
        if i == SUBLANES - 2:
            size = half * SUBLANES
            copy = pltpu.make_async_copy(
                tile_ref.at[pl.ds(block * size, size)],
                o_ref.at[at_ref[0], pl.ds((block * parts + part) * size, size)],
                sems.at[block],
            )
            copy.start()
            copies.append(copy)
    for copy in copies:
        copy.wait()


def multiply_last(at, part, parts, integrals, th, tl, ladder):
    b_width, depth = integrals.shape[2:]
    held = pl.BlockSpec(memory_space=pltpu.VMEM)
    anywhere = pl.BlockSpec(memory_space=pl.ANY)
    products = b_width * depth * NI * NO
    return pl.pallas_call(
        functools.partial(last_kernel, part, parts),
        out_shape=jax.ShapeDtypeStruct(ladder.shape, ladder.dtype),
        in_specs=[pl.BlockSpec(memory_space=pltpu.SMEM), held, held, held, anywhere],
        out_specs=anywhere,
        scratch_shapes=[
            pltpu.VMEM((2 * b_width, depth), jnp.bfloat16),
            pltpu.VMEM((NI * NO // LANES, b_width, LANES), jnp.float32),
            pltpu.VMEM((NI * NO * b_width // LANES, LANES), jnp.float32),
            pltpu.SemaphoreType.DMA((NI // SUBLANES,)),
        ],
        input_output_aliases={4: 0},
        compiler_params=pltpu.CompilerParams(vmem_limit_bytes=24 << 20),
        cost_estimate=pl.CostEstimate(
            flops=6 * products,
            bytes_accessed=4 * (integrals.size + b_width * NI * NO),
            transcendentals=0,
        ),
    )(at.reshape(1), integrals, th, tl, ladder)


def gather_over(axis, pieces, masks):
    size = lax.axis_size(axis)
    here = lax.axis_index(axis)
    held = {0: pieces}
    for mask in masks:
        sent = sorted(held)
        block = jnp.concatenate([held[k] for k in sent]) if len(sent) > 1 else held[sent[0]]
        got = lax.ppermute(block, axis, [(k, k ^ mask) for k in range(size)])
        each = pieces.shape[0]
        for n, k in enumerate(sent):
            held[k ^ mask] = got[n * each : (n + 1) * each]
    stacked = jnp.stack([held[k] for k in range(size)])
    bit = 1
    while bit < size:
        view = stacked.reshape((size // (2 * bit), 2, bit) + pieces.shape)
        stacked = jnp.where((here & bit) != 0, view[:, ::-1], view).reshape((size,) + pieces.shape)
        bit *= 2
    return stacked.reshape((size * pieces.shape[0],) + pieces.shape[1:])


def gather_amplitudes(amplitudes):
    cols, rows = lax.axis_size("col"), lax.axis_size("row")
    bits = [1 << k for k in range((cols - 1).bit_length())]
    masks = ([cols - 1] + bits[:-1]) if cols > 1 else []
    pieces = gather_over("col", amplitudes[None], masks)
    pieces = gather_over("row", pieces, [1 << k for k in range((rows - 1).bit_length())])
    each = amplitudes.shape[1] // NO
    panel = pieces.reshape(-1, NC, NI, each, NO).transpose(1, 0, 3, 2, 4)
    return panel.reshape(NC * NV, NI * NO)


def rounds_of(avals, cols):
    shifts = [s for pair in zip(range(1, cols), range(cols - 1, 0, -1)) for s in pair]
    shifts = list(dict.fromkeys(shifts))
    if avals < 16:
        sizes = [2] * (avals // 2 - 1) + [1, 1] if avals % 2 == 0 else [1] * avals
        return [[(shift, sum(sizes[:k]), sizes[k]) for shift in shifts] for k in range(len(sizes))]
    unit = avals // 16
    rounds = [[(shift, start * unit, count * unit) for shift in shifts] for start, count in ((0, 2), (2, 2), (4, 4))]
    rounds.append([(shift, 8 * unit, 8 * unit) for shift in shifts[:-1]] + [(shifts[-1], 8 * unit, 4 * unit)])
    rounds += [[(shifts[-1], start * unit, count * unit)] for start, count in ((12, 2), (14, 1), (15, 1))]
    return rounds


def body(integrals, amplitudes):
    cols = lax.axis_size("col")
    here = lax.axis_index("col")
    avals = integrals.shape[0] // NV
    b_width = NV // cols
    depth = integrals.shape[1]
    blocks = integrals.reshape(avals, cols, b_width, depth)

    arrived = []
    source = blocks
    for exchanges in rounds_of(avals, cols):
        parts = 2 if len(exchanges) == 1 and exchanges[0][2] == 1 else 1
        part_width = b_width // parts
        exchanges = [exchange + (part,) for exchange in exchanges for part in range(parts)]
        pieces = [
            lax.dynamic_slice(
                source,
                (start, (here + shift) % cols, part * part_width, 0),
                (count, 1, part_width, depth),
            )
            for shift, start, count, part in exchanges
        ]
        source, *pieces = lax.optimization_barrier((source, *pieces))
        for (shift, start, count, part), piece in zip(exchanges, pieces):
            got = lax.ppermute(piece, "col", [(k, (k + shift) % cols) for k in range(cols)])
            arrived.append(((here - shift) % cols * avals + start, part, parts, got))

    panel = gather_amplitudes(amplitudes)
    rounded = lax.reduce_precision(panel, 8, 7)
    th, tl = rounded.astype(jnp.bfloat16), (panel - rounded).astype(jnp.bfloat16)

    rows = cols * avals * NI
    out_shape = jax.ShapeDtypeStruct((cols * avals, NI * b_width * NO // LANES, LANES), jnp.float32)
    ladder = multiply(jnp.stack([here * avals, here]), blocks, th, tl, None, out_shape)
    for at, part, parts, got in arrived:
        if parts > 1:
            ladder = multiply_last(at, part, parts, got, th, tl, ladder)
        else:
            ladder = multiply(jnp.stack([at, jnp.zeros_like(at)]), got, th, tl, ladder, out_shape)
    ladder = ladder.reshape(rows // SUBLANES, b_width * NO // LANES, SUBLANES, LANES)
    return ladder.transpose(0, 2, 1, 3).reshape(rows, b_width * NO)


def solution(mesh):
    return jax.shard_map(
        body,
        mesh=mesh,
        in_specs=(P(("row", "col"), None), P(None, ("row", "col"))),
        out_specs=P("row", "col"),
        check_vma=False,
    )
```

```python
import functools

import jax
import jax.numpy as jnp
from jax import lax
from jax.experimental import pallas as pl
from jax.experimental.pallas import tpu as pltpu
from jax.sharding import PartitionSpec as P


NV = 512
NO = 64
NI = 32
NC = 2
LANES = 128
SUBLANES = 8


def split(values):
    high = values.astype(jnp.bfloat16)
    low = (values - high.astype(jnp.float32)).astype(jnp.bfloat16)
    return high, low


def ladder_kernel(group, width, at_ref, v_ref, th_ref, tl_ref, *refs):
    o_ref, vh_ref, vl_ref, part_ref = refs[-4:]
    b_width, depth = v_ref.shape[2:]
    half = b_width // 2
    rows = group * half
    vh_ref[...], vl_ref[...] = split(v_ref[...].reshape(group * b_width, depth))
    low_half = lax.broadcasted_iota(jnp.int32, (rows, LANES), 1) < NO

    def step(n, columns):
        th, tl = th_ref[:, columns], tl_ref[:, columns]
        vh, vl = vh_ref[...], vl_ref[...]
        dot = functools.partial(jnp.dot, preferred_element_type=jnp.float32)
        acc = dot(vh, tl) + dot(vl, th) + dot(vh, th)
        for pair in range(width // LANES):
            part_ref[pair] = acc[:, pair * LANES : (pair + 1) * LANES]
            even = part_ref[pair, pl.ds(0, rows, stride=2), :]
            odd = part_ref[pair, pl.ds(1, rows, stride=2), :]
            first = jnp.where(low_half, even, pltpu.roll(odd, NO, axis=1))
            second = jnp.where(low_half, pltpu.roll(even, NO, axis=1), odd)
            block, i = divmod(2 * pair, SUBLANES)
            at = (n * (width // (SUBLANES * NO)) + block) * half * SUBLANES + i
            for a in range(group):
                o_ref[a, pl.ds(at, half, stride=SUBLANES), :] = first[a * half : (a + 1) * half]
                o_ref[a, pl.ds(at + 1, half, stride=SUBLANES), :] = second[a * half : (a + 1) * half]

    steps = NI * NO // width
    if steps == 1:
        step(0, slice(None))
    else:

        @pl.loop(0, steps)
        def _(n):
            step(n, pl.ds(pl.multiple_of(n * width, width), width))


def multiply(at, integrals, th, tl, ladder, out_shape):
    avals, _, b_width, depth = integrals.shape
    group = 2 if avals % 2 == 0 else 1
    width = SUBLANES * NO
    aliased = ladder is not None
    spec = pl.BlockSpec((depth, NI * NO), lambda g, at: (0, 0), pipeline_mode=pl.Buffered(1))
    products = avals * b_width * depth * NI * NO
    return pl.pallas_call(
        functools.partial(ladder_kernel, group, width),
        out_shape=out_shape,
        grid_spec=pltpu.PrefetchScalarGridSpec(
            num_scalar_prefetch=1,
            grid=(avals // group,),
            in_specs=[
                pl.BlockSpec((group, 1, b_width, depth), lambda g, at: (g, at[1], 0, 0)),
                spec,
                spec,
            ]
            + [pl.BlockSpec(memory_space=pl.ANY)] * aliased,
            out_specs=pl.BlockSpec((group,) + out_shape.shape[1:], lambda g, at: (at[0] // group + g, 0, 0)),
            scratch_shapes=[pltpu.VMEM((group * b_width, depth), jnp.bfloat16)] * 2
            + [pltpu.VMEM((width // LANES, group * b_width, LANES), jnp.float32)],
        ),
        input_output_aliases={4: 0} if aliased else {},
        compiler_params=pltpu.CompilerParams(vmem_limit_bytes=32 << 20),
        cost_estimate=pl.CostEstimate(
            flops=6 * products,
            bytes_accessed=4 * (integrals.size + avals * b_width * NI * NO + depth * NI * NO),
            transcendentals=0,
        ),
    )(at, integrals, th, tl, *([ladder] if aliased else []))


def part_products(part, v_ref, th_ref, tl_ref, vs_ref):
    b_width, depth = v_ref.shape[2:]
    vs_ref[:b_width, :], vs_ref[b_width:, :] = split(v_ref[...].reshape(b_width, depth))
    rows = slice(part * depth, (part + 1) * depth)
    dot = functools.partial(jnp.dot, preferred_element_type=jnp.float32)
    both = dot(vs_ref[...], th_ref[rows, :])
    return dot(vs_ref[:b_width, :], tl_ref[rows, :]) + both[b_width:] + both[:b_width]


def first_kernel(v_ref, th_ref, tl_ref, _, sum_ref, __, vs_ref):
    sum_ref[...] = part_products(0, v_ref, th_ref, tl_ref, vs_ref)


def last_kernel(at_ref, v_ref, th_ref, tl_ref, sum_ref, _, o_ref, vs_ref, part_ref, tile_ref, sems):
    half = v_ref.shape[2] // 2
    acc = part_products(1, v_ref, th_ref, tl_ref, vs_ref)
    low_half = lax.broadcasted_iota(jnp.int32, (half, LANES), 1) < NO
    copies = []
    for pair in range(NI * NO // LANES):
        columns = slice(pair * LANES, (pair + 1) * LANES)
        part_ref[pair] = acc[:, columns] + sum_ref[:, columns]
        even = part_ref[pair, pl.ds(0, half, stride=2), :]
        odd = part_ref[pair, pl.ds(1, half, stride=2), :]
        block, i = divmod(2 * pair, SUBLANES)
        at = block * half * SUBLANES + i
        tile_ref[pl.ds(at, half, stride=SUBLANES), :] = jnp.where(low_half, even, pltpu.roll(odd, NO, axis=1))
        tile_ref[pl.ds(at + 1, half, stride=SUBLANES), :] = jnp.where(low_half, pltpu.roll(even, NO, axis=1), odd)
        if i == SUBLANES - 2:
            place = pl.ds(block * half * SUBLANES, half * SUBLANES)
            copy = pltpu.make_async_copy(tile_ref.at[place], o_ref.at[at_ref[0], place], sems.at[block])
            copy.start()
            copies.append(copy)
    for copy in copies:
        copy.wait()


def multiply_last(at, parts, th, tl, ladder):
    b_width, depth = parts[0].shape[2:]
    held = pl.BlockSpec(memory_space=pltpu.VMEM)
    anywhere = pl.BlockSpec(memory_space=pl.ANY)
    cost = pl.CostEstimate(
        flops=6 * b_width * depth * NI * NO,
        bytes_accessed=4 * b_width * (depth + NI * NO),
        transcendentals=0,
    )
    stacked = pltpu.VMEM((2 * b_width, depth), jnp.bfloat16)
    params = pltpu.CompilerParams(vmem_limit_bytes=24 << 20)
    written = jax.ShapeDtypeStruct(ladder.shape, ladder.dtype)
    sums, ladder = pl.pallas_call(
        first_kernel,
        out_shape=(jax.ShapeDtypeStruct((b_width, NI * NO), jnp.float32), written),
        in_specs=[held, held, held, anywhere],
        out_specs=(held, anywhere),
        scratch_shapes=[stacked],
        input_output_aliases={3: 1},
        compiler_params=params,
        cost_estimate=cost,
    )(parts[0], th, tl, ladder)
    return pl.pallas_call(
        last_kernel,
        out_shape=written,
        in_specs=[pl.BlockSpec(memory_space=pltpu.SMEM), held, held, held, held, anywhere],
        out_specs=anywhere,
        scratch_shapes=[
            stacked,
            pltpu.VMEM((NI * NO // LANES, b_width, LANES), jnp.float32),
            pltpu.VMEM((NI * NO * b_width // LANES, LANES), jnp.float32),
            pltpu.SemaphoreType.DMA((NI // SUBLANES,)),
        ],
        input_output_aliases={5: 0},
        compiler_params=params,
        cost_estimate=cost,
    )(at.reshape(1), parts[1], th, tl, sums, ladder)


def gather_over(axis, pieces, masks):
    size = lax.axis_size(axis)
    here = lax.axis_index(axis)
    held = {0: pieces}
    for mask in masks:
        sent = sorted(held)
        block = jnp.concatenate([held[k] for k in sent]) if len(sent) > 1 else held[sent[0]]
        got = lax.ppermute(block, axis, [(k, k ^ mask) for k in range(size)])
        each = pieces.shape[0]
        for n, k in enumerate(sent):
            held[k ^ mask] = got[n * each : (n + 1) * each]
    stacked = jnp.stack([held[k] for k in range(size)])
    bit = 1
    while bit < size:
        view = stacked.reshape((size // (2 * bit), 2, bit) + pieces.shape)
        stacked = jnp.where((here & bit) != 0, view[:, ::-1], view).reshape((size,) + pieces.shape)
        bit *= 2
    return stacked.reshape((size * pieces.shape[0],) + pieces.shape[1:])


def gather_amplitudes(amplitudes):
    cols, rows = lax.axis_size("col"), lax.axis_size("row")
    bits = [1 << k for k in range((cols - 1).bit_length())]
    masks = ([cols - 1] + bits[:-1]) if cols > 1 else []
    pieces = gather_over("col", amplitudes[None], masks)
    pieces = gather_over("row", pieces, [1 << k for k in range((rows - 1).bit_length())])
    each = amplitudes.shape[1] // NO
    panel = pieces.reshape(-1, NC, NI, each, NO).transpose(1, 0, 3, 2, 4)
    return panel.reshape(NC * NV, NI * NO)


def rounds_of(avals, cols):
    shifts = [s for pair in zip(range(1, cols), range(cols - 1, 0, -1)) for s in pair]
    shifts = list(dict.fromkeys(shifts))
    if avals < 16:
        sizes = [2] * (avals // 2 - 1) + [1, 1] if avals % 2 == 0 else [1] * avals
        return [[(shift, sum(sizes[:k]), sizes[k]) for shift in shifts] for k in range(len(sizes))]
    unit = avals // 16
    rounds = [[(shift, start * unit, count * unit) for shift in shifts] for start, count in ((0, 2), (2, 2), (4, 4))]
    rounds.append([(shift, 8 * unit, 8 * unit) for shift in shifts[:-1]] + [(shifts[-1], 8 * unit, 4 * unit)])
    rounds += [[(shifts[-1], start * unit, count * unit)] for start, count in ((12, 2), (14, 1), (15, 1))]
    return rounds


def body(integrals, amplitudes):
    cols = lax.axis_size("col")
    here = lax.axis_index("col")
    avals = integrals.shape[0] // NV
    b_width = NV // cols
    depth = integrals.shape[1]
    blocks = integrals.reshape(avals, cols, b_width, depth)

    arrived = []
    source = blocks
    for exchanges in rounds_of(avals, cols):
        parts = 2 if len(exchanges) == 1 and exchanges[0][2] == 1 else 1
        width = depth // parts
        sent = [exchange + (part,) for exchange in exchanges for part in range(parts)]
        pieces = [
            lax.dynamic_slice(
                source,
                (start, (here + shift) % cols, 0, part * width),
                (count, 1, b_width, width),
            )
            for shift, start, count, part in sent
        ]
        source, *pieces = lax.optimization_barrier((source, *pieces))
        got = [
            lax.ppermute(piece, "col", [(k, (k + shift) % cols) for k in range(cols)])
            for (shift, *_), piece in zip(sent, pieces)
        ]
        for n, (shift, start, _) in enumerate(exchanges):
            arrived.append(((here - shift) % cols * avals + start, got[n * parts : (n + 1) * parts]))

    panel = gather_amplitudes(amplitudes)
    rounded = lax.reduce_precision(panel, 8, 7)
    th, tl = rounded.astype(jnp.bfloat16), (panel - rounded).astype(jnp.bfloat16)

    rows = cols * avals * NI
    out_shape = jax.ShapeDtypeStruct((cols * avals, NI * b_width * NO // LANES, LANES), jnp.float32)
    ladder = multiply(jnp.stack([here * avals, here]), blocks, th, tl, None, out_shape)
    for at, parts in arrived:
        if len(parts) > 1:
            ladder = multiply_last(at, parts, th, tl, ladder)
        else:
            ladder = multiply(jnp.stack([at, jnp.zeros_like(at)]), parts[0], th, tl, ladder, out_shape)
    ladder = ladder.reshape(rows // SUBLANES, b_width * NO // LANES, SUBLANES, LANES)
    return ladder.transpose(0, 2, 1, 3).reshape(rows, b_width * NO)


def solution(mesh):
    return jax.shard_map(
        body,
        mesh=mesh,
        in_specs=(P(("row", "col"), None), P(None, ("row", "col"))),
        out_specs=P("row", "col"),
        check_vma=False,
    )
```

```python
import functools

import jax
import jax.numpy as jnp
from jax import lax
from jax.experimental import pallas as pl
from jax.experimental.pallas import tpu as pltpu
from jax.sharding import PartitionSpec as P


NV = 512
NO = 64
NI = 32
NC = 2
LANES = 128
SUBLANES = 8


def split(values):
    high = values.astype(jnp.bfloat16)
    low = (values - high.astype(jnp.float32)).astype(jnp.bfloat16)
    return high, low


def ladder_kernel(group, width, at_ref, v_ref, th_ref, tl_ref, *refs):
    o_ref, vh_ref, vl_ref, part_ref = refs[-4:]
    b_width, depth = v_ref.shape[2:]
    half = b_width // 2
    rows = group * half
    vh_ref[...], vl_ref[...] = split(v_ref[...].reshape(group * b_width, depth))
    low_half = lax.broadcasted_iota(jnp.int32, (rows, LANES), 1) < NO

    def step(n, columns):
        th, tl = th_ref[:, columns], tl_ref[:, columns]
        vh, vl = vh_ref[...], vl_ref[...]
        dot = functools.partial(jnp.dot, preferred_element_type=jnp.float32)
        acc = dot(vh, tl) + dot(vl, th) + dot(vh, th)
        for pair in range(width // LANES):
            part_ref[pair] = acc[:, pair * LANES : (pair + 1) * LANES]
            even = part_ref[pair, pl.ds(0, rows, stride=2), :]
            odd = part_ref[pair, pl.ds(1, rows, stride=2), :]
            first = jnp.where(low_half, even, pltpu.roll(odd, NO, axis=1))
            second = jnp.where(low_half, pltpu.roll(even, NO, axis=1), odd)
            block, i = divmod(2 * pair, SUBLANES)
            at = (n * (width // (SUBLANES * NO)) + block) * half * SUBLANES + i
            for a in range(group):
                o_ref[a, pl.ds(at, half, stride=SUBLANES), :] = first[a * half : (a + 1) * half]
                o_ref[a, pl.ds(at + 1, half, stride=SUBLANES), :] = second[a * half : (a + 1) * half]

    steps = NI * NO // width
    if steps == 1:
        step(0, slice(None))
    else:

        @pl.loop(0, steps)
        def _(n):
            step(n, pl.ds(pl.multiple_of(n * width, width), width))


def multiply(at, integrals, th, tl, ladder, out_shape):
    avals, _, b_width, depth = integrals.shape
    group = 2 if avals % 2 == 0 else 1
    width = SUBLANES * NO
    aliased = ladder is not None
    spec = pl.BlockSpec((depth, NI * NO), lambda g, at: (0, 0), pipeline_mode=pl.Buffered(1))
    products = avals * b_width * depth * NI * NO
    return pl.pallas_call(
        functools.partial(ladder_kernel, group, width),
        out_shape=out_shape,
        grid_spec=pltpu.PrefetchScalarGridSpec(
            num_scalar_prefetch=1,
            grid=(avals // group,),
            in_specs=[
                pl.BlockSpec((group, 1, b_width, depth), lambda g, at: (g, at[1], 0, 0)),
                spec,
                spec,
            ]
            + [pl.BlockSpec(memory_space=pl.ANY)] * aliased,
            out_specs=pl.BlockSpec((group,) + out_shape.shape[1:], lambda g, at: (at[0] // group + g, 0, 0)),
            scratch_shapes=[pltpu.VMEM((group * b_width, depth), jnp.bfloat16)] * 2
            + [pltpu.VMEM((width // LANES, group * b_width, LANES), jnp.float32)],
        ),
        input_output_aliases={4: 0} if aliased else {},
        compiler_params=pltpu.CompilerParams(vmem_limit_bytes=32 << 20),
        cost_estimate=pl.CostEstimate(
            flops=6 * products,
            bytes_accessed=4 * (integrals.size + avals * b_width * NI * NO + depth * NI * NO),
            transcendentals=0,
        ),
    )(at, integrals, th, tl, *([ladder] if aliased else []))


def part_products(part, v_ref, th_ref, tl_ref, vs_ref):
    b_width, depth = v_ref.shape[2:]
    vs_ref[:b_width, :], vs_ref[b_width:, :] = split(v_ref[...].reshape(b_width, depth))
    rows = slice(part * depth, (part + 1) * depth)
    dot = functools.partial(jnp.dot, preferred_element_type=jnp.float32)
    both = dot(vs_ref[...], th_ref[rows, :])
    return dot(vs_ref[:b_width, :], tl_ref[rows, :]) + both[b_width:] + both[:b_width]


def sum_kernel(part, v_ref, th_ref, tl_ref, *refs):
    sum_ref, _, vs_ref = refs[-3:]
    acc = part_products(part, v_ref, th_ref, tl_ref, vs_ref)
    sum_ref[...] = acc if part == 0 else acc + refs[0][...]


def last_kernel(part, at_ref, v_ref, th_ref, tl_ref, sum_ref, _, o_ref, vs_ref, part_ref, tile_ref, sems):
    half = v_ref.shape[2] // 2
    acc = part_products(part, v_ref, th_ref, tl_ref, vs_ref)
    low_half = lax.broadcasted_iota(jnp.int32, (half, LANES), 1) < NO
    copies = []
    for pair in range(NI * NO // LANES):
        columns = slice(pair * LANES, (pair + 1) * LANES)
        part_ref[pair] = acc[:, columns] + sum_ref[:, columns]
        even = part_ref[pair, pl.ds(0, half, stride=2), :]
        odd = part_ref[pair, pl.ds(1, half, stride=2), :]
        block, i = divmod(2 * pair, SUBLANES)
        at = block * half * SUBLANES + i
        tile_ref[pl.ds(at, half, stride=SUBLANES), :] = jnp.where(low_half, even, pltpu.roll(odd, NO, axis=1))
        tile_ref[pl.ds(at + 1, half, stride=SUBLANES), :] = jnp.where(low_half, pltpu.roll(even, NO, axis=1), odd)
        if i == SUBLANES - 2:
            place = pl.ds(block * half * SUBLANES, half * SUBLANES)
            copy = pltpu.make_async_copy(tile_ref.at[place], o_ref.at[at_ref[0], place], sems.at[block])
            copy.start()
            copies.append(copy)
    for copy in copies:
        copy.wait()


def multiply_last(at, parts, th, tl, ladder):
    b_width, depth = parts[0].shape[2:]
    held = pl.BlockSpec(memory_space=pltpu.VMEM)
    anywhere = pl.BlockSpec(memory_space=pl.ANY)
    cost = pl.CostEstimate(
        flops=6 * b_width * depth * NI * NO,
        bytes_accessed=4 * b_width * (depth + NI * NO),
        transcendentals=0,
    )
    stacked = pltpu.VMEM((2 * b_width, depth), jnp.bfloat16)
    params = pltpu.CompilerParams(vmem_limit_bytes=24 << 20)
    written = jax.ShapeDtypeStruct(ladder.shape, ladder.dtype)
    sums = []
    for part, piece in enumerate(parts[:-1]):
        *sums, ladder = pl.pallas_call(
            functools.partial(sum_kernel, part),
            out_shape=(jax.ShapeDtypeStruct((b_width, NI * NO), jnp.float32), written),
            in_specs=[held] * (3 + len(sums)) + [anywhere],
            out_specs=(held, anywhere),
            scratch_shapes=[stacked],
            input_output_aliases={3 + len(sums): 1},
            compiler_params=params,
            cost_estimate=cost,
        )(piece, th, tl, *sums, ladder)
    return pl.pallas_call(
        functools.partial(last_kernel, len(parts) - 1),
        out_shape=written,
        in_specs=[pl.BlockSpec(memory_space=pltpu.SMEM), held, held, held, held, anywhere],
        out_specs=anywhere,
        scratch_shapes=[
            stacked,
            pltpu.VMEM((NI * NO // LANES, b_width, LANES), jnp.float32),
            pltpu.VMEM((NI * NO * b_width // LANES, LANES), jnp.float32),
            pltpu.SemaphoreType.DMA((NI // SUBLANES,)),
        ],
        input_output_aliases={5: 0},
        compiler_params=params,
        cost_estimate=cost,
    )(at.reshape(1), parts[-1], th, tl, *sums, ladder)


def gather_over(axis, pieces, masks):
    size = lax.axis_size(axis)
    here = lax.axis_index(axis)
    held = {0: pieces}
    for mask in masks:
        sent = sorted(held)
        block = jnp.concatenate([held[k] for k in sent]) if len(sent) > 1 else held[sent[0]]
        got = lax.ppermute(block, axis, [(k, k ^ mask) for k in range(size)])
        each = pieces.shape[0]
        for n, k in enumerate(sent):
            held[k ^ mask] = got[n * each : (n + 1) * each]
    stacked = jnp.stack([held[k] for k in range(size)])
    bit = 1
    while bit < size:
        view = stacked.reshape((size // (2 * bit), 2, bit) + pieces.shape)
        stacked = jnp.where((here & bit) != 0, view[:, ::-1], view).reshape((size,) + pieces.shape)
        bit *= 2
    return stacked.reshape((size * pieces.shape[0],) + pieces.shape[1:])


def gather_amplitudes(amplitudes):
    cols, rows = lax.axis_size("col"), lax.axis_size("row")
    bits = [1 << k for k in range((cols - 1).bit_length())]
    masks = ([cols - 1] + bits[:-1]) if cols > 1 else []
    pieces = gather_over("col", amplitudes[None], masks)
    pieces = gather_over("row", pieces, [1 << k for k in range((rows - 1).bit_length())])
    each = amplitudes.shape[1] // NO
    panel = pieces.reshape(-1, NC, NI, each, NO).transpose(1, 0, 3, 2, 4)
    return panel.reshape(NC * NV, NI * NO)


def rounds_of(avals, cols):
    shifts = [s for pair in zip(range(1, cols), range(cols - 1, 0, -1)) for s in pair]
    shifts = list(dict.fromkeys(shifts))
    if avals < 16:
        sizes = [2] * (avals // 2 - 1) + [1, 1] if avals % 2 == 0 else [1] * avals
        return [[(shift, sum(sizes[:k]), sizes[k]) for shift in shifts] for k in range(len(sizes))]
    unit = avals // 16
    rounds = [[(shift, start * unit, count * unit) for shift in shifts] for start, count in ((0, 2), (2, 2), (4, 4))]
    rounds.append([(shift, 8 * unit, 8 * unit) for shift in shifts[:-1]] + [(shifts[-1], 8 * unit, 4 * unit)])
    rounds += [[(shifts[-1], start * unit, count * unit)] for start, count in ((12, 2), (14, 1), (15, 1))]
    return rounds


def body(integrals, amplitudes):
    cols = lax.axis_size("col")
    here = lax.axis_index("col")
    avals = integrals.shape[0] // NV
    b_width = NV // cols
    depth = integrals.shape[1]
    blocks = integrals.reshape(avals, cols, b_width, depth)

    arrived = []
    source = blocks
    for exchanges in rounds_of(avals, cols):
        parts = 1
        if len(exchanges) == 1 and exchanges[0][2] == 1:
            parts = 4 if exchanges[0][1] == avals - 1 else 2
        width = depth // parts
        sent = [exchange + (part,) for exchange in exchanges for part in range(parts)]
        pieces = [
            lax.dynamic_slice(
                source,
                (start, (here + shift) % cols, 0, part * width),
                (count, 1, b_width, width),
            )
            for shift, start, count, part in sent
        ]
        source, *pieces = lax.optimization_barrier((source, *pieces))
        got = [
            lax.ppermute(piece, "col", [(k, (k + shift) % cols) for k in range(cols)])
            for (shift, *_), piece in zip(sent, pieces)
        ]
        for n, (shift, start, _) in enumerate(exchanges):
            arrived.append(((here - shift) % cols * avals + start, got[n * parts : (n + 1) * parts]))

    panel = gather_amplitudes(amplitudes)
    rounded = lax.reduce_precision(panel, 8, 7)
    th, tl = rounded.astype(jnp.bfloat16), (panel - rounded).astype(jnp.bfloat16)

    rows = cols * avals * NI
    out_shape = jax.ShapeDtypeStruct((cols * avals, NI * b_width * NO // LANES, LANES), jnp.float32)
    ladder = multiply(jnp.stack([here * avals, here]), blocks, th, tl, None, out_shape)
    for at, parts in arrived:
        if len(parts) > 1:
            ladder = multiply_last(at, parts, th, tl, ladder)
        else:
            ladder = multiply(jnp.stack([at, jnp.zeros_like(at)]), parts[0], th, tl, ladder, out_shape)
    ladder = ladder.reshape(rows // SUBLANES, b_width * NO // LANES, SUBLANES, LANES)
    return ladder.transpose(0, 2, 1, 3).reshape(rows, b_width * NO)


def solution(mesh):
    return jax.shard_map(
        body,
        mesh=mesh,
        in_specs=(P(("row", "col"), None), P(None, ("row", "col"))),
        out_specs=P("row", "col"),
        check_vma=False,
    )
```

```python
import functools

import jax
import jax.numpy as jnp
from jax import lax
from jax.experimental import pallas as pl
from jax.experimental.pallas import tpu as pltpu
from jax.sharding import PartitionSpec as P


NV = 512
NO = 64
NI = 32
NC = 2
LANES = 128
SUBLANES = 8


def split(values):
    high = values.astype(jnp.bfloat16)
    low = (values - high.astype(jnp.float32)).astype(jnp.bfloat16)
    return high, low


def ladder_kernel(group, width, at_ref, v_ref, th_ref, tl_ref, *refs):
    o_ref, vh_ref, vl_ref, part_ref = refs[-4:]
    b_width, depth = v_ref.shape[2:]
    half = b_width // 2
    rows = group * half
    vh_ref[...], vl_ref[...] = split(v_ref[...].reshape(group * b_width, depth))
    low_half = lax.broadcasted_iota(jnp.int32, (rows, LANES), 1) < NO

    def step(n, columns):
        th, tl = th_ref[:, columns], tl_ref[:, columns]
        vh, vl = vh_ref[...], vl_ref[...]
        dot = functools.partial(jnp.dot, preferred_element_type=jnp.float32)
        acc = dot(vh, tl) + dot(vl, th) + dot(vh, th)
        for pair in range(width // LANES):
            part_ref[pair] = acc[:, pair * LANES : (pair + 1) * LANES]
            even = part_ref[pair, pl.ds(0, rows, stride=2), :]
            odd = part_ref[pair, pl.ds(1, rows, stride=2), :]
            first = jnp.where(low_half, even, pltpu.roll(odd, NO, axis=1))
            second = jnp.where(low_half, pltpu.roll(even, NO, axis=1), odd)
            block, i = divmod(2 * pair, SUBLANES)
            at = (n * (width // (SUBLANES * NO)) + block) * half * SUBLANES + i
            for a in range(group):
                o_ref[a, pl.ds(at, half, stride=SUBLANES), :] = first[a * half : (a + 1) * half]
                o_ref[a, pl.ds(at + 1, half, stride=SUBLANES), :] = second[a * half : (a + 1) * half]

    steps = NI * NO // width
    if steps == 1:
        step(0, slice(None))
    else:

        @pl.loop(0, steps)
        def _(n):
            step(n, pl.ds(pl.multiple_of(n * width, width), width))


def multiply(at, integrals, th, tl, ladder, out_shape):
    avals, _, b_width, depth = integrals.shape
    group = 2 if avals % 2 == 0 else 1
    width = SUBLANES * NO
    aliased = ladder is not None
    spec = pl.BlockSpec((depth, NI * NO), lambda g, at: (0, 0), pipeline_mode=pl.Buffered(1))
    products = avals * b_width * depth * NI * NO
    return pl.pallas_call(
        functools.partial(ladder_kernel, group, width),
        out_shape=out_shape,
        grid_spec=pltpu.PrefetchScalarGridSpec(
            num_scalar_prefetch=1,
            grid=(avals // group,),
            in_specs=[
                pl.BlockSpec((group, 1, b_width, depth), lambda g, at: (g, at[1], 0, 0)),
                spec,
                spec,
            ]
            + [pl.BlockSpec(memory_space=pl.ANY)] * aliased,
            out_specs=pl.BlockSpec((group,) + out_shape.shape[1:], lambda g, at: (at[0] // group + g, 0, 0)),
            scratch_shapes=[pltpu.VMEM((group * b_width, depth), jnp.bfloat16)] * 2
            + [pltpu.VMEM((width // LANES, group * b_width, LANES), jnp.float32)],
        ),
        input_output_aliases={4: 0} if aliased else {},
        compiler_params=pltpu.CompilerParams(vmem_limit_bytes=32 << 20),
        cost_estimate=pl.CostEstimate(
            flops=6 * products,
            bytes_accessed=4 * (integrals.size + avals * b_width * NI * NO + depth * NI * NO),
            transcendentals=0,
        ),
    )(at, integrals, th, tl, *([ladder] if aliased else []))


def stack_halves(v_ref, vs_ref):
    b_width, depth = v_ref.shape[2:]
    vs_ref[:b_width, :], vs_ref[b_width:, :] = split(v_ref[...].reshape(b_width, depth))


def part_products(part, columns, vs_ref, th_ref, tl_ref):
    b_width, depth = vs_ref.shape[0] // 2, vs_ref.shape[1]
    rows = slice(part * depth, (part + 1) * depth)
    dot = functools.partial(jnp.dot, preferred_element_type=jnp.float32)
    both = dot(vs_ref[...], th_ref[rows, columns])
    return dot(vs_ref[:b_width, :], tl_ref[rows, columns]) + both[b_width:] + both[:b_width]


def sum_kernel(part, v_ref, th_ref, tl_ref, *refs):
    sum_ref, _, vs_ref = refs[-3:]
    stack_halves(v_ref, vs_ref)
    acc = part_products(part, slice(None), vs_ref, th_ref, tl_ref)
    sum_ref[...] = acc if part == 0 else acc + refs[0][...]


def last_kernel(part, at_ref, v_ref, th_ref, tl_ref, sum_ref, _, o_ref, vs_ref, part_ref, tile_ref, sems):
    half = v_ref.shape[2] // 2
    stack_halves(v_ref, vs_ref)
    width = SUBLANES * NO
    low_half = lax.broadcasted_iota(jnp.int32, (half, LANES), 1) < NO
    copies = []
    for pair in range(NI * NO // LANES):
        if pair * LANES % width == 0:
            acc = part_products(part, slice(pair * LANES, pair * LANES + width), vs_ref, th_ref, tl_ref)
        columns = slice(pair * LANES, (pair + 1) * LANES)
        inner = pair * LANES % width
        part_ref[pair] = acc[:, inner : inner + LANES] + sum_ref[:, columns]
        even = part_ref[pair, pl.ds(0, half, stride=2), :]
        odd = part_ref[pair, pl.ds(1, half, stride=2), :]
        block, i = divmod(2 * pair, SUBLANES)
        at = block * half * SUBLANES + i
        tile_ref[pl.ds(at, half, stride=SUBLANES), :] = jnp.where(low_half, even, pltpu.roll(odd, NO, axis=1))
        tile_ref[pl.ds(at + 1, half, stride=SUBLANES), :] = jnp.where(low_half, pltpu.roll(even, NO, axis=1), odd)
        if i == SUBLANES - 2:
            place = pl.ds(block * half * SUBLANES, half * SUBLANES)
            copy = pltpu.make_async_copy(tile_ref.at[place], o_ref.at[at_ref[0], place], sems.at[block])
            copy.start()
            copies.append(copy)
    for copy in copies:
        copy.wait()


def multiply_last(at, parts, th, tl, ladder):
    b_width, depth = parts[0].shape[2:]
    held = pl.BlockSpec(memory_space=pltpu.VMEM)
    anywhere = pl.BlockSpec(memory_space=pl.ANY)
    cost = pl.CostEstimate(
        flops=6 * b_width * depth * NI * NO,
        bytes_accessed=4 * b_width * (depth + NI * NO),
        transcendentals=0,
    )
    stacked = pltpu.VMEM((2 * b_width, depth), jnp.bfloat16)
    params = pltpu.CompilerParams(vmem_limit_bytes=24 << 20)
    written = jax.ShapeDtypeStruct(ladder.shape, ladder.dtype)
    sums = []
    for part, piece in enumerate(parts[:-1]):
        *sums, ladder = pl.pallas_call(
            functools.partial(sum_kernel, part),
            out_shape=(jax.ShapeDtypeStruct((b_width, NI * NO), jnp.float32), written),
            in_specs=[held] * (3 + len(sums)) + [anywhere],
            out_specs=(held, anywhere),
            scratch_shapes=[stacked],
            input_output_aliases={3 + len(sums): 1},
            compiler_params=params,
            cost_estimate=cost,
        )(piece, th, tl, *sums, ladder)
    return pl.pallas_call(
        functools.partial(last_kernel, len(parts) - 1),
        out_shape=written,
        in_specs=[pl.BlockSpec(memory_space=pltpu.SMEM), held, held, held, held, anywhere],
        out_specs=anywhere,
        scratch_shapes=[
            stacked,
            pltpu.VMEM((NI * NO // LANES, b_width, LANES), jnp.float32),
            pltpu.VMEM((NI * NO * b_width // LANES, LANES), jnp.float32),
            pltpu.SemaphoreType.DMA((NI // SUBLANES,)),
        ],
        input_output_aliases={5: 0},
        compiler_params=params,
        cost_estimate=cost,
    )(at.reshape(1), parts[-1], th, tl, *sums, ladder)


def gather_over(axis, pieces, masks):
    size = lax.axis_size(axis)
    here = lax.axis_index(axis)
    held = {0: pieces}
    for mask in masks:
        sent = sorted(held)
        block = jnp.concatenate([held[k] for k in sent]) if len(sent) > 1 else held[sent[0]]
        got = lax.ppermute(block, axis, [(k, k ^ mask) for k in range(size)])
        each = pieces.shape[0]
        for n, k in enumerate(sent):
            held[k ^ mask] = got[n * each : (n + 1) * each]
    stacked = jnp.stack([held[k] for k in range(size)])
    bit = 1
    while bit < size:
        view = stacked.reshape((size // (2 * bit), 2, bit) + pieces.shape)
        stacked = jnp.where((here & bit) != 0, view[:, ::-1], view).reshape((size,) + pieces.shape)
        bit *= 2
    return stacked.reshape((size * pieces.shape[0],) + pieces.shape[1:])


def gather_amplitudes(amplitudes):
    cols, rows = lax.axis_size("col"), lax.axis_size("row")
    bits = [1 << k for k in range((cols - 1).bit_length())]
    masks = ([cols - 1] + bits[:-1]) if cols > 1 else []
    pieces = gather_over("col", amplitudes[None], masks)
    pieces = gather_over("row", pieces, [1 << k for k in range((rows - 1).bit_length())])
    each = amplitudes.shape[1] // NO
    panel = pieces.reshape(-1, NC, NI, each, NO).transpose(1, 0, 3, 2, 4)
    return panel.reshape(NC * NV, NI * NO)


def rounds_of(avals, cols):
    shifts = [s for pair in zip(range(1, cols), range(cols - 1, 0, -1)) for s in pair]
    shifts = list(dict.fromkeys(shifts))
    if avals < 16:
        sizes = [2] * (avals // 2 - 1) + [1, 1] if avals % 2 == 0 else [1] * avals
        return [[(shift, sum(sizes[:k]), sizes[k]) for shift in shifts] for k in range(len(sizes))]
    unit = avals // 16
    rounds = [[(shift, start * unit, count * unit) for shift in shifts] for start, count in ((0, 2), (2, 2), (4, 4))]
    rounds.append([(shift, 8 * unit, 8 * unit) for shift in shifts[:-1]] + [(shifts[-1], 8 * unit, 4 * unit)])
    rounds += [[(shifts[-1], start * unit, count * unit)] for start, count in ((12, 2), (14, 1), (15, 1))]
    return rounds


def body(integrals, amplitudes):
    cols = lax.axis_size("col")
    here = lax.axis_index("col")
    avals = integrals.shape[0] // NV
    b_width = NV // cols
    depth = integrals.shape[1]
    blocks = integrals.reshape(avals, cols, b_width, depth)

    arrived = []
    source = blocks
    for exchanges in rounds_of(avals, cols):
        parts = 1
        if len(exchanges) == 1 and exchanges[0][2] == 1:
            parts = 4 if exchanges[0][1] == avals - 1 else 2
        width = depth // parts
        sent = [exchange + (part,) for exchange in exchanges for part in range(parts)]
        pieces = [
            lax.dynamic_slice(
                source,
                (start, (here + shift) % cols, 0, part * width),
                (count, 1, b_width, width),
            )
            for shift, start, count, part in sent
        ]
        source, *pieces = lax.optimization_barrier((source, *pieces))
        got = [
            lax.ppermute(piece, "col", [(k, (k + shift) % cols) for k in range(cols)])
            for (shift, *_), piece in zip(sent, pieces)
        ]
        for n, (shift, start, _) in enumerate(exchanges):
            arrived.append(((here - shift) % cols * avals + start, got[n * parts : (n + 1) * parts]))

    panel = gather_amplitudes(amplitudes)
    rounded = lax.reduce_precision(panel, 8, 7)
    th, tl = rounded.astype(jnp.bfloat16), (panel - rounded).astype(jnp.bfloat16)

    rows = cols * avals * NI
    out_shape = jax.ShapeDtypeStruct((cols * avals, NI * b_width * NO // LANES, LANES), jnp.float32)
    ladder = multiply(jnp.stack([here * avals, here]), blocks, th, tl, None, out_shape)
    for at, parts in arrived:
        if len(parts) > 1:
            ladder = multiply_last(at, parts, th, tl, ladder)
        else:
            ladder = multiply(jnp.stack([at, jnp.zeros_like(at)]), parts[0], th, tl, ladder, out_shape)
    ladder = ladder.reshape(rows // SUBLANES, b_width * NO // LANES, SUBLANES, LANES)
    return ladder.transpose(0, 2, 1, 3).reshape(rows, b_width * NO)


def solution(mesh):
    return jax.shard_map(
        body,
        mesh=mesh,
        in_specs=(P(("row", "col"), None), P(None, ("row", "col"))),
        out_specs=P("row", "col"),
        check_vma=False,
    )
```
